32 devices in a mesh: segment: 4 (over y, core), lane: 2 (over x), dp: 4 (over z).
Axes of the slice: x: 2, y: 2, z: 4, core: 2. Of those that a mesh axis runs over, the one named last changes fastest.
Arguments:
- inputs: bfloat16 [4, 2, 256, 3072], P('segment', None, 'dp', 'lane'), may hold values from -6 to 6
- gate_sums: bfloat16 [4, 2, 256, 1632], P('segment', None, 'dp', 'lane'), may hold values from -6 to 6
- top_grads: bfloat16 [2, 256, 3072], P(None, 'dp', 'lane'), may hold values from -6 to 6
- up_weight: bfloat16 [4, 3072, 1632], P('segment', None, 'lane'), may hold values from -0.109375 to 0.109375
- down_weight: bfloat16 [4, 1632, 3072], P('segment', 'lane'), may hold values from -0.15625 to 0.15625
- projectors: bfloat16 [4, 2, 1632, 128], P('segment', None, 'lane'), may hold values from -1 to 1, as said below
- first_moment: float32 [4, 2, 2, 128, 3072], P('segment', 'lane', None, None, 'dp'), may hold values from -6 to 6
- second_moment: float32 [4, 2, 2, 128, 3072], P('segment', 'lane', None, None, 'dp'), may hold values from 10.24 to 256
Outputs:
- input_grads: bfloat16 [4, 2, 256, 3072], P('segment', None, 'dp', 'lane')
- new_first: float32 [4, 2, 2, 128, 3072], P('segment', 'lane', None, None, 'dp')
- new_second: float32 [4, 2, 2, 128, 3072], P('segment', 'lane', None, None, 'dp')
- new_up: bfloat16 [4, 3072, 1632], P('segment', 'dp', 'lane')
- new_down: bfloat16 [4, 1632, 3072], P('segment', 'lane', 'dp')
The draws below stay inside these ranges and needn't reach their ends.
Inputs may be any that keep to these rules, and one draw needn't show every extreme that they name: For every section, kind and lane, the 816 rows of projectors that belong to that lane form a matrix with orthonormal columns, up to bfloat16 rounding.
All inputs are finite; a program needn't handle non-finite values.
Results may differ from the reference program's by a relative error of at most 0.018.
Values may be sent and summed in bfloat16 or wider, within the bound.
No kernel may reach another device: no remote copies, remote signals or barrier semaphores. Data moves between devices by JAX's collectives and lax.ppermute only.
A program may use at most 64 MiB of HBM per device.

```python
import math
import jax
import jax.numpy as jnp
from jax import lax

D = 3072
FF_DEV = 816
RANK = 128
M = 2
SEGMENTS = 4
LANES = 2
TOKENS = 256
FF = 1632


def draw_projectors(key, part):
    gaussian = jax.random.normal(jax.random.fold_in(key, 7), (SEGMENTS, 2, LANES, FF_DEV, RANK), jnp.float32)
    ortho_basis, upper_part = jnp.linalg.qr(gaussian)
    return ortho_basis.reshape(SEGMENTS, 2, LANES * FF_DEV, RANK).astype(jnp.bfloat16)


def with_spikes(array, key, source, target, shards_of, factor):
    def block_of(position):
        return (jnp.arange(array.shape[position]) // (array.shape[position] // shards_of)).reshape((-1,) + (1,) * (array.ndim - 1 - position))

    one_side = jax.random.permutation(key, shards_of)[block_of(target)]
    far = (block_of(target) + shards_of // 2) % shards_of
    return jnp.where((block_of(source) == one_side) | (block_of(source) == far), factor * array, array)


def levels(key, extent, shards, low, high):
    level, own = 1.0, jax.random.fold_in(key, 6)
    for axis_at, blocks in shards:
        draws = jnp.exp(jax.random.uniform(jax.random.fold_in(own, axis_at), (blocks,), jnp.float32, low / len(shards), high / len(shards)))
        level = level * jnp.repeat(draws, extent[axis_at] // blocks).reshape([-1 if axis == axis_at else 1 for axis in range(len(extent))])
    return level


def scatter_about(stream_key, dims, spread, most, pieces=(), kind=jnp.bfloat16):
    entries = spread * jax.random.normal(stream_key, dims, jnp.float32)
    if pieces:
        entries = entries * levels(stream_key, dims, pieces, -0.22, 0.18)
    return jnp.clip(entries, -most, most).astype(kind)


def noise_with(own_key, shape, deviation, limit, pieces, heavy, kind=jnp.bfloat16):
    values = deviation * jax.random.normal(own_key, shape, jnp.float32)
    if pieces:
        values = values * levels(own_key, shape, pieces, -0.22, 0.18)
    return jnp.clip(with_spikes(values, jax.random.fold_in(own_key, 3), *heavy), -limit, limit).astype(kind)


def setup_inputs(seed: int = 0) -> dict:
    streams_of = jax.random.split(jax.random.key(seed), 9)
    return {
        "inputs": noise_with(streams_of[0], (SEGMENTS, M, TOKENS, D), 1.0, 6.0, ((0, 4), (2, 4), (3, 2)), (2, 3, 4, 2.0)),
        "gate_sums": scatter_about(streams_of[1], (SEGMENTS, M, TOKENS, FF), 1.0, 6.0, ((0, 4), (2, 4), (3, 2))),
        "top_grads": scatter_about(streams_of[2], (M, TOKENS, D), 1.0, 6.0, ((1, 4), (2, 2))),
        "up_weight": scatter_about(streams_of[3], (SEGMENTS, D, FF), D ** -0.5, 0.109375, ((0, 4), (2, 2))),
        "down_weight": scatter_about(streams_of[4], (SEGMENTS, FF, D), FF ** -0.5, 0.15625, ((0, 4), (1, 2))),
        "projectors": draw_projectors(jax.random.fold_in(streams_of[8], 71), 0),
        "first_moment": scatter_about(streams_of[6], (SEGMENTS, LANES, 2, RANK, D), (0.1 * (M * TOKENS) ** 0.5), 6.0, ((0, 4), (1, 2), (4, 4)), jnp.float32),
        "second_moment": jnp.clip(jnp.exp(math.log(256.0) - 3.218876 * jax.random.uniform(streams_of[7], (SEGMENTS, LANES, 2, RANK, D), jnp.float32) ** levels(streams_of[7], (SEGMENTS, LANES, 2, RANK, D), ((0, 4), (1, 2), (4, 4)), -0.2, 0.2)), 10.24, 256.0),
    }


def reference(inputs, gate_sums, top_grads, up_weight, down_weight, projectors, first_moment, second_moment):
    grads_by_segment = [None] * SEGMENTS
    first_by_segment = [None] * SEGMENTS
    second_by_segment = [None] * SEGMENTS
    up_by_segment = [None] * SEGMENTS
    down_by_segment = [None] * SEGMENTS
    cotangents = top_grads
    contract_cols = (((1,), (1,)), ((), ()))
    contract_rows = (((0,), (0,)), ((), ()))
    for segment_index in reversed(range(SEGMENTS)):
        weight_up = up_weight[segment_index]
        weight_down = down_weight[segment_index]
        proj_up = projectors[segment_index, 0]
        proj_down = projectors[segment_index, 1]
        code_total = jnp.zeros((LANES, 2, RANK, D), jnp.float32)
        segment_grads = []
        for micro_index in range(M):
            cotangent = cotangents[micro_index]
            input_rows = inputs[segment_index, micro_index]
            up_value = jnp.dot(input_rows.astype(jnp.float32), weight_up.astype(jnp.float32), preferred_element_type=jnp.float32)
            gate_act = jax.nn.silu(gate_sums[segment_index, micro_index].astype(jnp.float32))
            hidden = (gate_act * up_value).astype(jnp.bfloat16)
            hidden_grad = lax.dot_general(cotangent.astype(jnp.float32), weight_down.astype(jnp.float32), contract_cols, preferred_element_type=jnp.float32)
            up_grad = (hidden_grad * gate_act).astype(jnp.bfloat16)
            summed = cotangent.astype(jnp.float32)
            for lane_index in range(LANES):
                low = lane_index * FF_DEV
                high = low + FF_DEV
                part = lax.dot_general(up_grad[:, low:high].astype(jnp.float32), weight_up[:, low:high].astype(jnp.float32), contract_cols, preferred_element_type=jnp.float32)
                part = lax.optimization_barrier(part.astype(jnp.bfloat16))
                summed = summed + part.astype(jnp.float32)
                code_up = jnp.dot(up_grad[:, low:high].astype(jnp.float32), proj_up[low:high].astype(jnp.float32), preferred_element_type=jnp.float32).astype(jnp.bfloat16)
                code_down = jnp.dot(hidden[:, low:high].astype(jnp.float32), proj_down[low:high].astype(jnp.float32), preferred_element_type=jnp.float32).astype(jnp.bfloat16)
                term_up = lax.dot_general(code_up.astype(jnp.float32), input_rows.astype(jnp.float32), contract_rows, preferred_element_type=jnp.float32)
                term_down = lax.dot_general(code_down.astype(jnp.float32), cotangent.astype(jnp.float32), contract_rows, preferred_element_type=jnp.float32)
                code_total = code_total.at[lane_index].add(jnp.stack([term_up, term_down]))
            segment_grads.append(summed.astype(jnp.bfloat16))
        segment_grads = jnp.stack(segment_grads)
        grads_by_segment[segment_index] = segment_grads
        cotangents = segment_grads
        first_next = 0.9 * first_moment[segment_index] + 0.1 * code_total
        second_next = 0.999 * second_moment[segment_index] + 0.001 * code_total * code_total
        step_code = first_next / (jnp.sqrt(second_next) + 1e-08)
        first_by_segment[segment_index] = first_next
        second_by_segment[segment_index] = second_next
        up_blocks = []
        down_blocks = []
        for lane_index in range(LANES):
            low = lane_index * FF_DEV
            high = low + FF_DEV
            delta_up = lax.dot_general(step_code[lane_index, 0], proj_up[low:high].astype(jnp.float32), (((0,), (1,)), ((), ())), precision=lax.Precision.HIGHEST)
            up_blocks.append((weight_up[:, low:high].astype(jnp.float32) - 0.05 * delta_up).astype(jnp.bfloat16))
            delta_down = jnp.dot(proj_down[low:high].astype(jnp.float32), step_code[lane_index, 1], precision=lax.Precision.HIGHEST)
            down_blocks.append((weight_down[low:high].astype(jnp.float32) - 0.05 * delta_down).astype(jnp.bfloat16))
        up_by_segment[segment_index] = jnp.concatenate(up_blocks, axis=1)
        down_by_segment[segment_index] = jnp.concatenate(down_blocks, axis=0)
    return (jnp.stack(grads_by_segment), jnp.stack(first_by_segment), jnp.stack(second_by_segment), jnp.stack(up_by_segment), jnp.stack(down_by_segment))
```

```python
import functools

import jax
import jax.numpy as jnp
from jax import lax
from jax.experimental import pallas as pl
from jax.experimental.pallas import tpu as pltpu
from jax.sharding import PartitionSpec as P

AXES = ("segment", "lane", "dp")
DIRECT_GROUPS = 8
NT = (((1,), (1,)), ((), ()))
TN = (((0,), (0,)), ((), ()))


def send(value, move, segments):
    lanes, groups = lax.axis_size("lane"), lax.axis_size("dp")
    pairs = []
    for s in segments:
        for l in range(lanes):
            for d in range(groups):
                ts, tl, td = move(s, l, d)
                pairs.append(((s * lanes + l) * groups + d, (ts * lanes + tl) * groups + td))
    return lax.ppermute(value, AXES, pairs)


def silu(v):
    return v / (1.0 + jnp.exp(-v))


def columns(ref, index, width):
    return ref[:, pl.ds(pl.multiple_of(index * width, 128), width)]


def call(kernel, name, at, operands, outs, scratch=(), smem=True):
    vmem = pl.BlockSpec(memory_space=pltpu.VMEM)
    return pl.pallas_call(
        kernel,
        name=name,
        in_specs=[pl.BlockSpec(memory_space=pltpu.SMEM)] + [vmem] * len(operands),
        out_specs=[vmem] * len(outs),
        out_shape=[jax.ShapeDtypeStruct(s, t) for s, t in outs],
        scratch_shapes=list(scratch),
    )(at, *operands)


def tick(at, segment, lanes, groups, first, last, pieces, gates, weight_down, weight_up_t, proj, prior):
    rows, hid = gates.shape
    width = weight_down.shape[1]
    half = width // lanes
    part = width // groups
    rank = proj.shape[1]
    bf = jnp.bfloat16
    n_piece = len(pieces)
    n_prior = len(prior)
    slices = groups if groups <= DIRECT_GROUPS else 1
    slice_width = part if slices == groups else width
    outs = [((rows, rank), bf), ((rows, half), bf)] + [((rows, slice_width), bf)] * slices
    if last:
        outs = outs + [((rows, half), bf)] * lanes
    else:
        outs = outs + [((rows, width), bf)] * 2

    def kernel(at_ref, *refs):
        piece = refs[:n_piece]
        gate_ref, down_ref, up_ref, proj_ref = refs[n_piece : n_piece + 4]
        prior_refs = refs[n_piece + 4 : n_piece + 4 + n_prior]
        out = refs[n_piece + 4 + n_prior : -1]
        cot = refs[-1]
        active = at_ref[0] == segment
        lane, group = at_ref[1], at_ref[2]
        if first:
            for k in range(lanes):
                place = lax.rem(lane - k + lanes, lanes)
                value = piece[k][...]
                cot[:, pl.ds(pl.multiple_of(place * half, 128), half)] = jnp.where(
                    active, value, jnp.zeros_like(value)
                )
        else:
            total = piece[0][...].astype(jnp.float32)
            for other in piece[1:]:
                total = total + other[...].astype(jnp.float32)
            cot[...] = total.astype(bf)
        code_ref, half_ref = out[0], out[1]
        slice_refs = out[2 : 2 + slices]
        rest = out[2 + slices :]
        own_half = columns(cot, lane, half)
        cuts = [
            columns(cot, lax.rem(group + k, groups), part) if slices == groups else cot[...]
            for k in range(slices)
        ]
        if n_prior:
            own_half = own_half + prior_refs[1][...]
            cuts = [c + prior_refs[2 + k][...] for k, c in enumerate(cuts)]
        half_ref[...] = own_half
        for k in range(slices):
            slice_refs[k][...] = cuts[k]
        act = silu(gate_ref[...].astype(jnp.float32))
        hidden_grad = lax.dot_general(cot[...], down_ref[...], NT, preferred_element_type=jnp.float32)
        up_grad = (hidden_grad * act).astype(bf)
        share = jnp.dot(up_grad, up_ref[...], preferred_element_type=jnp.float32)
        code = jnp.dot(up_grad, proj_ref[...], preferred_element_type=jnp.float32).astype(bf)
        if n_prior:
            code = code + prior_refs[0][...]
        code_ref[...] = code
        if last:
            cot[...] = (cot[...].astype(jnp.float32) + share).astype(bf)
            rest[0][...] = columns(cot, lane, half)
            cot[...] = share.astype(bf)
            for k in range(1, lanes):
                rest[k][...] = columns(cot, lax.rem(lane + k, lanes), half)
        else:
            rest[0][...] = (cot[...].astype(jnp.float32) + share).astype(bf)
            rest[1][...] = share.astype(bf)

    return call(
        kernel,
        f"tick{segment}",
        at,
        [*pieces, gates, weight_down, weight_up_t, proj, *prior],
        outs,
        [pltpu.VMEM((rows, width), bf)],
    )


def hidden_codes(at, lanes, groups, pieces, gates, weight_up_t, proj):
    rows, hid = gates.shape
    width = weight_up_t.shape[1]
    half = width // lanes
    part = width // groups
    rank = proj.shape[1]
    bf = jnp.bfloat16
    slices = groups if groups <= DIRECT_GROUPS else 1
    slice_width = part if slices == groups else width

    def kernel(at_ref, *refs):
        piece = refs[:lanes]
        gate_ref, up_ref, proj_ref = refs[lanes : lanes + 3]
        out = refs[lanes + 3 : -1]
        full = refs[-1]
        lane, group = at_ref[1], at_ref[2]
        for k in range(lanes):
            place = lax.rem(lane - k + lanes, lanes)
            full[:, pl.ds(pl.multiple_of(place * half, 128), half)] = piece[k][...]
        for k in range(slices):
            if slices == groups:
                out[1 + k][...] = columns(full, lax.rem(group + k, groups), part)
            else:
                out[1 + k][...] = full[...]
        value = lax.dot_general(full[...], up_ref[...], NT, preferred_element_type=jnp.float32)
        hidden = (silu(gate_ref[...].astype(jnp.float32)) * value).astype(bf)
        out[0][...] = jnp.dot(hidden, proj_ref[...], preferred_element_type=jnp.float32).astype(bf)

    return call(
        kernel,
        "hidden",
        at,
        [*pieces, gates, weight_up_t, proj],
        [((rows, rank), bf)] + [((rows, slice_width), bf)] * slices,
        [pltpu.VMEM((rows, width), bf)],
    )


def adam(code_sum, first, second):
    first_next = 0.9 * first + 0.1 * code_sum
    second_next = 0.999 * second + 0.001 * code_sum * code_sum
    return first_next, second_next, first_next / (jnp.sqrt(second_next) + 1e-08)


def update(at, codes, rows, proj, weight, first, second):
    count = len(codes)
    group_sizes = [len(r) for r in rows]
    flat = [x for r in rows for x in r]
    rank, width = first.shape
    hid = weight.shape[0]
    block = 256 if width % 256 == 0 else width
    steps = width // block

    def kernel(at_ref, *refs):
        code_refs = refs[:count]
        row_refs = refs[count : count + len(flat)]
        proj_ref, weight_ref, first_ref, second_ref, first_out, second_out, weight_out = refs[
            count + len(flat) :
        ]
        total = jnp.zeros((rank, block), jnp.float32)
        at_row = 0
        for j in range(count):
            value = row_refs[at_row][...]
            for i in range(1, group_sizes[j]):
                value = value + row_refs[at_row + i][...]
            at_row += group_sizes[j]
            total = total + lax.dot_general(
                code_refs[j][...], value, TN, preferred_element_type=jnp.float32
            )
        first_next, second_next, step = adam(total, first_ref[...], second_ref[...])
        first_out[...] = first_next
        second_out[...] = second_next
        delta = jnp.dot(
            proj_ref[...], step.astype(jnp.bfloat16), preferred_element_type=jnp.float32
        )
        weight_out[...] = (weight_ref[...].astype(jnp.float32) - 0.05 * delta).astype(jnp.bfloat16)

    def whole(x):
        return pl.BlockSpec(x.shape, lambda j, at_ref: (0, 0))

    def col(x):
        return pl.BlockSpec((x.shape[0], block), lambda j, at_ref: (0, j))

    return pl.pallas_call(
        kernel,
        name="update",
        grid_spec=pltpu.PrefetchScalarGridSpec(
            num_scalar_prefetch=1,
            grid=(steps,),
            in_specs=[whole(c) for c in codes]
            + [col(r) for r in flat]
            + [
                whole(proj),
                pl.BlockSpec((hid, block), lambda j, at_ref: (0, at_ref[2] * steps + j)),
                col(first),
                col(second),
            ],
            out_specs=[col(first), col(second), pl.BlockSpec((hid, block), lambda j, at_ref: (0, j))],
        ),
        out_shape=[
            jax.ShapeDtypeStruct(first.shape, jnp.float32),
            jax.ShapeDtypeStruct(second.shape, jnp.float32),
            jax.ShapeDtypeStruct((hid, width), jnp.bfloat16),
        ],
    )(at, *codes, *flat, proj, weight, first, second)


def update_wide(codes, rows, proj, weight, first, second):
    total = lax.dot_general(codes, rows, TN, preferred_element_type=jnp.float32)
    first_next, second_next, step = adam(total, first, second)
    own = lax.dynamic_slice_in_dim(
        weight, lax.axis_index("dp") * first.shape[1], first.shape[1], 1
    )
    delta = jnp.dot(proj, step.astype(jnp.bfloat16), preferred_element_type=jnp.float32)
    return first_next, second_next, (own.astype(jnp.float32) - 0.05 * delta).astype(jnp.bfloat16)


def local(
    inputs, gate_sums, top_grads, up_weight, down_weight, projectors, first_moment, second_moment
):
    segments, lanes, groups = (lax.axis_size(a) for a in AXES)
    at = jnp.stack([lax.axis_index(a) for a in AXES]).astype(jnp.int32)
    micros, rows, half = top_grads.shape
    weight_up_t = up_weight[0].T
    weight_down = down_weight[0]
    proj_up, proj_down = projectors[0, 0], projectors[0, 1]
    direct = groups <= DIRECT_GROUPS and first_moment.shape[4] % 128 == 0
    everyone = range(segments)
    shifts = range(1, groups) if direct else ()

    def lane_move(k, step=0):
        return lambda s, l, d: (s + step, (l + k) % lanes, d)

    def group_move(k):
        return lambda s, l, d: (s, l, (d + k) % groups)

    pieces = []
    for m in range(micros):
        own = top_grads[m]
        pieces.append(
            [own] + [send(own, lane_move(k), [segments - 1]) for k in range(1, lanes)]
        )
    prior = [()] * micros
    moved = [[] for _ in shifts]
    kept = []
    for t in range(segments):
        segment = segments - 1 - t
        last = segment == 0
        results = []
        for m in range(micros):
            out = tick(
                at, segment, lanes, groups, t == 0, last, pieces[m], gate_sums[0, m],
                weight_down, weight_up_t, proj_up, prior[m],
            )
            n_slice = groups if groups <= DIRECT_GROUPS else 1
            prior[m] = out[: 2 + n_slice]
            rest = out[2 + n_slice :]
            results.append(rest)
            if not last:
                pieces[m] = [
                    send(rest[0], lane_move(0, -1), [segment])
                ] + [send(rest[1], lane_move(k, -1), [segment]) for k in range(1, lanes)]
        if t == 1 or segments == 1:
            x_rows = inputs[0].reshape(micros * rows, half)
            x_pieces = [x_rows] + [send(x_rows, lane_move(k), everyone) for k in range(1, lanes)]
            hid_out = hidden_codes(
                at, lanes, groups, x_pieces, gate_sums[0].reshape(micros * rows, -1),
                weight_up_t, proj_down,
            )
            code_down, x_slices = hid_out[0], hid_out[1:]
            if direct:
                down_codes = [code_down] + [send(code_down, group_move(k), everyone) for k in shifts]
                x_moved = [x_slices[0]] + [
                    send(x_slices[k], group_move(k), everyone) for k in shifts
                ]
    code_up = jnp.concatenate([p[0] for p in prior], axis=0)
    halves = jnp.stack([p[1] for p in prior])
    back = send(halves, lambda s, l, d: (s + 1, l, d), range(segments - 1)) if segments > 1 else 0
    grads = jnp.stack([r[0] for r in results]).astype(jnp.float32)
    for k in range(1, lanes):
        grads = grads + send(jnp.stack([r[k] for r in results]), lane_move(k), [0]).astype(
            jnp.float32
        )
    out_grads = (grads + back).astype(jnp.bfloat16)
    first, second = first_moment[0, 0], second_moment[0, 0]
    if direct:
        up_codes = [code_up] + [send(code_up, group_move(k), everyone) for k in shifts]
        cots = [
            jnp.concatenate([p[2 + k] for p in prior], axis=0) for k in range(groups)
        ]
        cot_moved = [cots[0]] + [send(cots[k], group_move(k), everyone) for k in shifts]
        down = update(
            at, down_codes, [[c] for c in cot_moved], proj_down, weight_down, first[1], second[1]
        )
        up = update(at, up_codes, [[x] for x in x_moved], proj_up, weight_up_t, first[0], second[0])
    else:
        def spread(x):
            return lax.all_to_all(x, "dp", 1, 0, tiled=True)

        cot = jnp.concatenate([p[2] for p in prior], axis=0)
        down = update_wide(
            lax.all_gather(code_down, "dp", axis=0, tiled=True), spread(cot),
            proj_down, weight_down, first[1], second[1],
        )
        up = update_wide(
            lax.all_gather(code_up, "dp", axis=0, tiled=True), spread(x_slices[0]),
            proj_up, weight_up_t, first[0], second[0],
        )
    return (
        out_grads[None],
        jnp.stack([up[0], down[0]])[None, None],
        jnp.stack([up[1], down[1]])[None, None],
        up[2].T[None],
        down[2][None],
    )


def solution(mesh):
    placed = (
        P("segment", None, "dp", "lane"),
        P("segment", None, "dp", "lane"),
        P(None, "dp", "lane"),
        P("segment", None, "lane"),
        P("segment", "lane", None),
        P("segment", None, "lane", None),
        P("segment", "lane", None, None, "dp"),
        P("segment", "lane", None, None, "dp"),
    )
    return jax.shard_map(
        local,
        mesh=mesh,
        in_specs=placed,
        out_specs=(
            P("segment", None, "dp", "lane"),
            P("segment", "lane", None, None, "dp"),
            P("segment", "lane", None, None, "dp"),
            P("segment", "dp", "lane"),
            P("segment", "lane", "dp"),
        ),
        check_vma=False,
    )
```
